32 devices in a mesh: dp: 8 (over z, x), tensor: 4 (over y, core).
Axes of the slice: x: 2, y: 2, z: 4, core: 2. Of those that a mesh axis runs over, the one named last changes fastest.
Arguments:
- x_in: bfloat16 [4096, 1024], P('dp', 'tensor'), may hold values from -6 to 6
- cotangent: bfloat16 [4096, 1024], P('dp', 'tensor'), may hold values from -6 to 6
- seq_ids: int32 [4096], P('dp'), may hold values from -1 to 4095, as said below
- norm_gain: bfloat16 [1024], P('dp'), may hold values from 0.5 to 1.5
- w_zx: bfloat16 [1024, 2, 2048], P('dp', None, 'tensor'), may hold values from -0.1875 to 0.1875
- w_bc: bfloat16 [1024, 256], P('dp', 'tensor'), may hold values from -0.1875 to 0.1875
- w_dt: bfloat16 [1024, 32], P('dp', 'tensor'), may hold values from -0.1875 to 0.1875
- w_out_t: bfloat16 [1024, 2048], P('dp', 'tensor'), may hold values from -0.125 to 0.125
- conv_x_weight: float32 [4, 2048], P(None, 'tensor'), may hold values from -3 to 3
- conv_x_bias: float32 [2048], P('tensor'), may hold values from -3 to 3
- conv_bc_weight: float32 [4, 256], P(None, 'tensor'), may hold values from -3 to 3
- conv_bc_bias: float32 [256], P('tensor'), may hold values from -3 to 3
- dt_bias: float32 [32], P('tensor'), may hold values from -6.9 to -2.25
- a_log: float32 [32], P('tensor'), may hold values from 0 to 2.77
- d_skip: float32 [32], P('tensor'), may hold values from 0.5 to 1.5
- gate_gain: float32 [2048], P('tensor'), may hold values from 0.5 to 1.5
Outputs:
- output: bfloat16 [4096, 1024], P('dp', 'tensor')
- input_grad: float32 [4096, 1024], P('dp', 'tensor')
- grad_norm_gain: float32 [1024], P('dp')
- grad_w_zx: float32 [1024, 2, 2048], P('dp', None, 'tensor')
- grad_w_bc: float32 [1024, 256], P('dp', 'tensor')
- grad_w_dt: float32 [1024, 32], P('dp', 'tensor')
- grad_w_out_t: float32 [1024, 2048], P('dp', 'tensor')
- grad_conv_x_weight: float32 [4, 2048], P(None, 'tensor')
- grad_conv_x_bias: float32 [2048], P('tensor')
- grad_conv_bc_weight: float32 [4, 256], P(None, 'tensor')
- grad_conv_bc_bias: float32 [256], P('tensor')
- grad_dt_bias: float32 [32], P('tensor')
- grad_a_log: float32 [32], P('tensor')
- grad_d_skip: float32 [32], P('tensor')
- grad_gate_gain: float32 [2048], P('tensor')
The draws below stay inside these ranges and needn't reach their ends.
Inputs may be any that keep to these rules, and one draw needn't show every extreme that they name: `seq_ids`: each entry is -1 for an empty slot or the row index at which its sequence begins. In each block of 512 rows (the rows of one dp index) the live rows come first, their ids never fall, the empty slots follow, and every sequence lies inside one block; the last block has no empty slot and its last row begins a sequence of one row; some other blocks have empty slots.
All inputs are finite; a program needn't handle non-finite values.
Results may differ from the reference program's by a relative error of at most 0.017.
Values may be sent and summed in bfloat16 or wider, within the bound.
A program may use at most 128 MiB of HBM per device.

```python
from functools import partial
import jax
import jax.numpy as jnp
from jax import lax

D = 1024
HEADS = 32
STATE = 128
CONV = 4
GROUP = 256
CAP = 512
INNER = 2048
TOKENS = 4096
N_DP = 8


def draw_seq_ids(key, part):
    blocks = TOKENS // CAP
    key_fill, key_start = jax.random.split(key, 2)
    block_index = jnp.arange(blocks, dtype=jnp.int32)
    fills = jax.random.randint(key_fill, (blocks,), CAP // 8, CAP)
    fills = jnp.where(block_index == blocks - 1, CAP, fills)
    starts = jax.random.randint(key_start, (blocks, CAP), 0, 3 * GROUP) < 2
    position = jnp.arange(CAP, dtype=jnp.int32)
    final_start = (block_index[:, None] == blocks - 1) & (position[None, :] == CAP - 1)
    starts = starts | (position[None, :] == 0) | final_start
    marks = jnp.where(starts, position[None, :], 0)
    firsts = lax.cummax(marks, axis=1)
    ids = firsts + (block_index * CAP)[:, None]
    ids = jnp.where(position[None, :] < fills[:, None], ids, -1)
    return ids.reshape(-1).astype(jnp.int32)


def block_scale(rng, shape, cuts, least, top_value):
    loudness = 1.0
    for axis_at, blocks in cuts:
        steps = jax.random.uniform(jax.random.fold_in(jax.random.fold_in(rng, 6), axis_at), (blocks,), jnp.float32, least / len(cuts), top_value / len(cuts))
        loudness = loudness * jnp.repeat(jnp.exp(steps), shape[axis_at] // blocks).reshape((-1,) + (1,) * (len(shape) - 1 - axis_at))
    return loudness


def centred(rng, extent, scale, limit, cuts=(), held_as=jnp.bfloat16):
    level = block_scale(rng, extent, cuts, -0.22, 0.18) if cuts else 1.0
    array = jax.random.normal(rng, extent, jnp.float32) * scale * level
    return jnp.minimum(jnp.maximum(array, -limit), limit).astype(held_as)


def setup_inputs(seed: int = 0) -> dict:
    splits = jax.random.split(jax.random.key(seed), 17)
    x_in = centred(splits[0], (TOKENS, D), 1.0, 6.0, ((0, 8), (1, 4)))
    cotangent = centred(splits[1], (TOKENS, D), 1.0, 6.0, ((0, 8), (1, 4)))
    seq_ids = draw_seq_ids(jax.random.fold_in(splits[16], 71), 0)
    norm_gain = jnp.clip(1.0 + 0.1 * jax.random.normal(splits[3], (D,), jnp.float32), 0.5, 1.5).astype(jnp.bfloat16)
    w_zx = centred(splits[4], (D, 2, INNER), D ** -0.5, 0.1875, ((0, 8), (2, 4)))
    w_bc = centred(splits[5], (D, 2 * STATE), D ** -0.5, 0.1875, ((0, 8), (1, 4)))
    w_dt = centred(splits[6], (D, HEADS), D ** -0.5, 0.1875, ((0, 8), (1, 4)))
    w_out_t = centred(splits[7], (D, INNER), INNER ** -0.5, 0.125, ((0, 8), (1, 4)))
    conv_x_weight = centred(splits[8], (CONV, INNER), CONV ** -0.5, 3.0, ((1, 4),), jnp.float32)
    conv_x_bias = centred(splits[9], (INNER,), 0.5, 3.0, ((0, 4),), jnp.float32)
    conv_bc_weight = centred(splits[10], (CONV, 2 * STATE), CONV ** -0.5, 3.0, ((1, 4),), jnp.float32)
    conv_bc_bias = centred(splits[11], (2 * STATE,), 0.5, 3.0, ((0, 4),), jnp.float32)
    dt_bias = jnp.clip(-6.9 + 4.65 * jax.random.uniform(splits[12], (HEADS,), jnp.float32) ** block_scale(splits[12], (HEADS,), ((0, 4),), -0.2, 0.2), -6.9, -2.25)
    a_log = jnp.clip(2.77 * jax.random.uniform(splits[13], (HEADS,), jnp.float32) ** block_scale(splits[13], (HEADS,), ((0, 4),), -0.2, 0.2), 0.0, 2.77)
    d_skip = jnp.clip(0.5 + 1.0 * jax.random.uniform(splits[14], (HEADS,), jnp.float32) ** block_scale(splits[14], (HEADS,), ((0, 4),), -0.2, 0.2), 0.5, 1.5)
    gate_gain = jnp.clip(1.0 + 0.1 * jax.random.normal(splits[15], (INNER,), jnp.float32), 0.5, 1.5)
    return {"x_in": x_in, "cotangent": cotangent, "seq_ids": seq_ids, "norm_gain": norm_gain, "w_zx": w_zx, "w_bc": w_bc, "w_dt": w_dt, "w_out_t": w_out_t, "conv_x_weight": conv_x_weight, "conv_x_bias": conv_x_bias, "conv_bc_weight": conv_bc_weight, "conv_bc_bias": conv_bc_bias, "dt_bias": dt_bias, "a_log": a_log, "d_skip": d_skip, "gate_gain": gate_gain}


EPSILON = 1e-05
PRECISE = lax.Precision.HIGHEST

def conv_silu(source, kernel, offset, segment):
    kernel_taps = kernel.shape[0]
    summed = offset[None, :] + kernel[kernel_taps - 1][None, :] * source
    for shift_rows in range(1, kernel_taps):
        shifted = jnp.concatenate([jnp.zeros((shift_rows, source.shape[1]), source.dtype), source[:-shift_rows]], axis=0)
        shifted_seg = jnp.concatenate([jnp.full((shift_rows,), -3, jnp.int32), segment[:-shift_rows].astype(jnp.int32)], axis=0)
        same_seg = (shifted_seg == segment.astype(jnp.int32)).astype(source.dtype)
        summed = summed + kernel[kernel_taps - 1 - shift_rows][None, :] * shifted * same_seg[:, None]
    return jax.nn.silu(summed)

def mixer_scan(inputs_x, b_matrix, c_matrix, dt_raw, dt_bias, a_log, d_skip, segment):
    row_count = inputs_x.shape[0]
    head_count = inputs_x.shape[1]
    groups = row_count // GROUP
    step_size = jax.nn.softplus(dt_raw + dt_bias[None, :])
    log_decay = -step_size * jnp.exp(a_log)[None, :]
    segment = segment.astype(jnp.int32)
    last_seg = segment[GROUP - 1::GROUP]
    prior_seg = jnp.concatenate([jnp.full((1,), -2, jnp.int32), last_seg[:-1]])
    blocked = (inputs_x.reshape(groups, GROUP, head_count, -1), b_matrix.reshape(groups, GROUP, -1), c_matrix.reshape(groups, GROUP, -1), step_size.reshape(groups, GROUP, head_count), log_decay.reshape(groups, GROUP, head_count), segment.reshape(groups, GROUP), prior_seg)
    causal = jnp.arange(GROUP)[:, None] >= jnp.arange(GROUP)[None, :]

    def advance(carry_state, pieces):
        x_blk, b_blk, c_blk, step_blk, decay_blk, seg_blk, prior = pieces
        cumulative = jnp.cumsum(decay_blk, axis=0)
        linked = causal & (seg_blk[:, None] == seg_blk[None, :])
        spread = cumulative[:, None, :] - cumulative[None, :, :]
        kernel_mat = jnp.where(linked[:, :, None], jnp.exp(jnp.minimum(spread, 0.0)), 0.0)
        scores = jnp.dot(c_blk, b_blk.T, precision=PRECISE)
        weights = scores[:, :, None] * kernel_mat * step_blk[None, :, :]
        y_diag = jnp.einsum('ijh,jhp->ihp', weights, x_blk, precision=PRECISE)
        entry_gate = jnp.exp(cumulative) * (seg_blk == prior).astype(cumulative.dtype)[:, None]
        y_carry = jnp.einsum('in,hnp->ihp', c_blk, carry_state, precision=PRECISE) * entry_gate[:, :, None]
        outputs = y_diag + y_carry + d_skip[None, :, None] * x_blk
        final_cum = cumulative[-1]
        tail_weight = jnp.exp(jnp.minimum(final_cum[None, :] - cumulative, 0.0)) * (seg_blk == seg_blk[-1]).astype(cumulative.dtype)[:, None] * step_blk
        retain = (seg_blk[-1] == prior).astype(cumulative.dtype)
        fresh_state = jnp.einsum('jn,jh,jhp->hnp', b_blk, tail_weight, x_blk, precision=PRECISE)
        return (retain * jnp.exp(final_cum)[:, None, None] * carry_state + fresh_state, outputs)
    zero_state = jnp.zeros((head_count, b_matrix.shape[1], inputs_x.shape[2]), inputs_x.dtype)
    final_state, mixed_out = lax.scan(advance, zero_state, blocked)
    return mixed_out.reshape(row_count, head_count, -1)

def silu_slope(value):
    logistic = jax.nn.sigmoid(value)
    return logistic * (1.0 + value * (1.0 - logistic))

def rows_product(left, right):
    return lax.dot_general(left, right, (((0,), (0,)), ((), ())), preferred_element_type=jnp.float32)

def cols_product(left, right):
    return lax.dot_general(left, right, (((1,), (1,)), ((), ())), preferred_element_type=jnp.float32)

def layer_block(x_rows, cot_rows, segment, norm_gain, w_zx, w_bc, w_dt, w_out_t, conv_x_weight, conv_x_bias, conv_bc_weight, conv_bc_bias, dt_bias, a_log, d_skip, gate_gain):
    row_count = x_rows.shape[0]
    inner_dim = w_out_t.shape[1]
    head_count = w_dt.shape[1]
    live_rows = (segment >= 0).astype(jnp.float32)
    x_float = x_rows.astype(jnp.float32)
    inv_rms = lax.rsqrt(lax.optimization_barrier(jnp.mean(x_float * x_float, axis=-1)) + EPSILON)
    gain_float = norm_gain.astype(jnp.float32)
    normed = (x_float * inv_rms[:, None] * gain_float[None, :]).astype(jnp.bfloat16)
    zx_flat = w_zx.reshape(w_zx.shape[0], -1)
    zx_proj = jnp.dot(normed, zx_flat, preferred_element_type=jnp.float32).astype(jnp.bfloat16)
    z_gate = zx_proj[:, :inner_dim]
    x_pre = zx_proj[:, inner_dim:]
    bc_pre = jnp.dot(normed, w_bc, preferred_element_type=jnp.float32).astype(jnp.bfloat16)
    dt_raw = jnp.dot(normed, w_dt, preferred_element_type=jnp.float32)
    conv_fn = partial(conv_silu, segment=segment)
    x_act, xconv_back = jax.vjp(conv_fn, x_pre.astype(jnp.float32), conv_x_weight, conv_x_bias)
    x_act = x_act.astype(jnp.bfloat16)
    bc_act, bcconv_back = jax.vjp(conv_fn, bc_pre.astype(jnp.float32), conv_bc_weight, conv_bc_bias)
    bc_act = bc_act.astype(jnp.bfloat16)
    state_dim = bc_act.shape[1] // 2
    mixer = partial(mixer_scan, segment=segment)
    y_heads, mixer_back = jax.vjp(mixer, x_act.astype(jnp.float32).reshape(row_count, head_count, -1), bc_act[:, :state_dim].astype(jnp.float32), bc_act[:, state_dim:].astype(jnp.float32), dt_raw, dt_bias, a_log, d_skip)
    y_flat = y_heads.reshape(row_count, inner_dim)
    z_float = z_gate.astype(jnp.float32)
    z_silu = jax.nn.silu(z_float)
    gated = y_flat * z_silu
    inv_gate = lax.rsqrt(lax.optimization_barrier(jnp.mean(gated * gated, axis=-1)) + EPSILON)
    q_rows = (gated * gate_gain[None, :]).astype(jnp.bfloat16)
    partial_out = cols_product(q_rows, w_out_t)
    output = (x_float + partial_out * (inv_gate * live_rows)[:, None]).astype(jnp.bfloat16)
    cot_float = cot_rows.astype(jnp.float32)
    d_scaled = (cot_float * (live_rows * inv_gate)[:, None]).astype(jnp.bfloat16)
    out_grad = rows_product(d_scaled, q_rows)
    d_q = jnp.dot(d_scaled, w_out_t, preferred_element_type=jnp.float32)
    row_dot = lax.optimization_barrier(jnp.sum(q_rows.astype(jnp.float32) * d_q, axis=-1))
    gate_grad = lax.optimization_barrier(jnp.sum(d_q * gated, axis=0))
    d_gated = d_q * gate_gain[None, :] - gated * (inv_gate * inv_gate * row_dot / inner_dim)[:, None]
    d_y = d_gated * z_silu
    d_z = d_gated * y_flat * silu_slope(z_float)
    dx_act, d_bmat, d_cmat, d_dtraw, dtbias_grad, alog_grad, dskip_grad = mixer_back(d_y.reshape(row_count, head_count, -1))
    d_xpre, xconv_grad, xbias_grad = xconv_back(dx_act.reshape(row_count, inner_dim))
    d_bcpre, bcconv_grad, bcbias_grad = bcconv_back(jnp.concatenate([d_bmat, d_cmat], axis=1))
    d_zx = jnp.concatenate([d_z, d_xpre], axis=1).astype(jnp.bfloat16)
    d_bc16 = d_bcpre.astype(jnp.bfloat16)
    d_dt16 = d_dtraw.astype(jnp.bfloat16)
    zx_grad = rows_product(normed, d_zx).reshape(w_zx.shape)
    bc_grad = rows_product(normed, d_bc16)
    dt_grad = rows_product(normed, d_dt16)
    d_norm = cols_product(d_zx, zx_flat) + cols_product(d_bc16, w_bc) + cols_product(d_dt16, w_dt)
    x_hat = x_float * inv_rms[:, None]
    gain_grad = lax.optimization_barrier(jnp.sum(d_norm * x_hat, axis=0))
    d_hat = d_norm * gain_float[None, :]
    input_grad = inv_rms[:, None] * (d_hat - x_hat * lax.optimization_barrier(jnp.mean(d_hat * x_hat, axis=-1))[:, None]) + cot_float
    return (output, input_grad, (gain_grad, zx_grad, bc_grad, dt_grad, out_grad, xconv_grad, xbias_grad, bcconv_grad, bcbias_grad, dtbias_grad, alog_grad, dskip_grad, gate_grad))

def reference(x_in, cotangent, seq_ids, norm_gain, w_zx, w_bc, w_dt, w_out_t, conv_x_weight, conv_x_bias, conv_bc_weight, conv_bc_bias, dt_bias, a_log, d_skip, gate_gain):
    params = (norm_gain, w_zx, w_bc, w_dt, w_out_t, conv_x_weight, conv_x_bias, conv_bc_weight, conv_bc_bias, dt_bias, a_log, d_skip, gate_gain)
    blocks = (x_in.reshape(N_DP, CAP, D), cotangent.reshape(N_DP, CAP, D), seq_ids.reshape(N_DP, CAP).astype(jnp.int32))

    def visit(totals, pieces):
        out_blk, grad_blk, block_grads = layer_block(pieces[0], pieces[1], pieces[2], *params)
        return (jax.tree.map(lambda a, b: a + b, totals, block_grads), (out_blk, grad_blk))
    zero_grads = tuple((jnp.zeros(p.shape, jnp.float32) for p in params))
    totals, stacked = lax.scan(visit, zero_grads, blocks)
    outputs = stacked[0].reshape(TOKENS, D)
    in_grads = stacked[1].reshape(TOKENS, D)
    return (outputs, in_grads, totals[0], totals[1], totals[2], totals[3], totals[4], totals[5], totals[6], totals[7], totals[8], totals[9], totals[10], totals[11], totals[12])
```

```python
from functools import partial
from types import SimpleNamespace

import jax
import jax.numpy as jnp
from jax import lax
from jax.experimental import pallas as pl
from jax.experimental.pallas import tpu as pltpu
from jax.sharding import PartitionSpec as P

HEAD_DIM = 64
PAIR = 2 * HEAD_DIM
EPSILON = 1e-05
PRECISE = lax.Precision.HIGHEST
F32 = jnp.float32
BF16 = jnp.bfloat16


def rows_product(left, right):
    return lax.dot_general(left, right, (((0,), (0,)), ((), ())), preferred_element_type=F32)


def cols_product(left, right):
    return lax.dot_general(left, right, (((1,), (1,)), ((), ())), preferred_element_type=F32)


def plain_product(left, right):
    return lax.dot_general(left, right, (((1,), (0,)), ((), ())), preferred_element_type=F32)


def conv_raw(source, taps, bias, masks):
    count = taps.shape[0]
    summed = bias + taps[count - 1 : count, :] * source
    for shift in range(1, count):
        summed = summed + taps[count - 1 - shift : count - shift, :] * (
            pltpu.roll(source, shift, 0) * masks[:, shift : shift + 1]
        )
    return summed


def conv_back(d_act, source, value, taps, masks):
    count = taps.shape[0]
    rows = source.shape[0]
    logistic = jax.nn.sigmoid(value)
    d_value = d_act * (logistic * (1.0 + value * (1.0 - logistic)))
    d_source = taps[count - 1 : count, :] * d_value
    tap_rows = [jnp.sum(d_value * source, axis=0, keepdims=True)]
    for shift in range(1, count):
        held = d_value * masks[:, shift : shift + 1]
        tap_rows.append(jnp.sum(held * pltpu.roll(source, shift, 0), axis=0, keepdims=True))
        d_source = d_source + taps[count - 1 - shift : count - shift, :] * pltpu.roll(
            held, rows - shift, 0
        )
    d_taps = jnp.concatenate(tap_rows[::-1], axis=0)
    return d_source, d_taps, jnp.sum(d_value, axis=0, keepdims=True)


def two_wide(columns, first):
    return jnp.where(first, columns[:, 0:1], columns[:, 1:2])


def forward_kernel(
    z_ref, x_ref, b_ref, c_ref, taps_ref, bias_ref, mask_ref, seg_ref, segt_ref,
    step_ref, cum_ref, cumt_ref, skip_ref, gain_ref, dq_ref,
    act_ref, y_ref, q_ref, stat_ref, scores,
):
    pair = pl.program_id(0)
    rows = z_ref.shape[0]
    half = rows // 2

    @pl.when(pair == 0)
    def _():
        full = cols_product(c_ref[...], b_ref[...])
        at_row = lax.broadcasted_iota(jnp.int32, full.shape, 0)
        at_col = lax.broadcasted_iota(jnp.int32, full.shape, 1)
        linked = (at_row >= at_col) & (seg_ref[...] == segt_ref[...])
        scores[...] = jnp.where(linked, full, 0.0)
        stat_ref[...] = jnp.zeros_like(stat_ref)

    value = conv_raw(x_ref[...].astype(F32), taps_ref[...], bias_ref[...], mask_ref[...])
    act = (value * jax.nn.sigmoid(value)).astype(BF16)
    act_ref[...] = act
    act_float = act.astype(F32)
    first = lax.broadcasted_iota(jnp.int32, act.shape, 1) < HEAD_DIM
    stepped = act_float * two_wide(step_ref[0], first)
    parts = (
        jnp.where(first, stepped, 0.0).astype(BF16),
        jnp.where(first, 0.0, stepped).astype(BF16),
    )
    for low, wide in ((0, half), (half, rows)):
        total = skip_ref[...] * act_float[low : low + half]
        for head in range(2):
            spread = (
                cum_ref[0, low : low + half, head : head + 1] - cumt_ref[0, head : head + 1, :wide]
            )
            weights = scores[low : low + half, :wide] * jnp.exp(jnp.minimum(spread, 0.0))
            total = total + plain_product(weights.astype(BF16), parts[head][:wide])
        y_ref[low : low + half, :] = total
    z_float = z_ref[...].astype(F32)
    gated = y_ref[...] * (z_float * jax.nn.sigmoid(z_float))
    q = (gated * gain_ref[...]).astype(BF16)
    q_ref[...] = q
    squares = jnp.sum(gated * gated, axis=1, keepdims=True)
    inner = jnp.sum(q.astype(F32) * dq_ref[...], axis=1, keepdims=True)
    pick = lax.broadcasted_iota(jnp.int32, stat_ref.shape, 1) == 0
    stat_ref[...] += jnp.where(pick, squares, inner)


def backward_kernel(
    z_ref, x_ref, b_ref, c_ref, taps_ref, bias_ref, mask_ref, seg_ref, segt_ref,
    step_ref, cum_ref, cumt_ref, skip_ref, gain_ref, dq_ref, act_ref, y_ref, scale_ref,
    dz_ref, dx_ref, dbc_ref, dtaps_ref, sums_ref, dstep_ref, rowsum_ref, colsum_ref,
    scores, d_scores,
):
    pair = pl.program_id(0)
    rows = z_ref.shape[0]
    half = rows // 2

    @pl.when(pair == 0)
    def _():
        full = cols_product(b_ref[...], c_ref[...])
        at_row = lax.broadcasted_iota(jnp.int32, full.shape, 0)
        at_col = lax.broadcasted_iota(jnp.int32, full.shape, 1)
        linked = (at_row <= at_col) & (seg_ref[...] == segt_ref[...])
        scores[...] = jnp.where(linked, full, 0.0)
        d_scores[...] = jnp.zeros_like(d_scores)

    z_float = z_ref[...].astype(F32)
    y = y_ref[...]
    logistic = jax.nn.sigmoid(z_float)
    z_silu = z_float * logistic
    gated = y * z_silu
    d_q = dq_ref[...] * scale_ref[:, 0:1]
    d_gated = d_q * gain_ref[...] - gated * scale_ref[:, 1:2]
    d_y = d_gated * z_silu
    dz_ref[...] = (d_gated * y * (logistic * (1.0 + z_float * (1.0 - logistic)))).astype(BF16)

    act = act_ref[...].astype(F32)
    first = lax.broadcasted_iota(jnp.int32, act.shape, 1) < HEAD_DIM
    step_wide = two_wide(step_ref[0], first)
    stepped = (act * step_wide).astype(BF16)
    parts = (
        jnp.where(first, d_y, 0.0).astype(BF16),
        jnp.where(first, 0.0, d_y).astype(BF16),
    )
    for low, start in ((0, 0), (half, half)):
        held = slice(low, low + half)
        total = jnp.zeros((half, PAIR), F32)
        for head in range(2):
            spread = cumt_ref[0, head : head + 1, start:] - cum_ref[0, held, head : head + 1]
            decay = jnp.exp(jnp.minimum(spread, 0.0))
            weights = scores[held, start:] * decay
            total = total + plain_product(weights.astype(BF16), parts[head][start:])
            d_weights = cols_product(stepped[held], parts[head][start:])
            d_scores[held, start:] += d_weights * decay
            d_spread = d_weights * weights
            colsum_ref[0, held, head : head + 1] = jnp.sum(d_spread, axis=1, keepdims=True)
            along = jnp.sum(d_spread, axis=0, keepdims=True)
            if low == 0:
                rowsum_ref[0, head : head + 1, :] = along
            else:
                rowsum_ref[0, head : head + 1, start:] += along
        direct = total * act[held]
        dstep_ref[0, held, 0:1] = jnp.sum(
            jnp.where(first[held], direct, 0.0), axis=1, keepdims=True
        )
        dstep_ref[0, held, 1:2] = jnp.sum(
            jnp.where(first[held], 0.0, direct), axis=1, keepdims=True
        )
        y_ref[held, :] = total * step_wide[held]
    d_act = y_ref[...] + skip_ref[...] * d_y
    source = x_ref[...].astype(F32)
    value = conv_raw(source, taps_ref[...], bias_ref[...], mask_ref[...])
    d_source, d_taps, d_bias = conv_back(d_act, source, value, taps_ref[...], mask_ref[...])
    dx_ref[...] = d_source.astype(BF16)
    dtaps_ref[...] = d_taps
    sums_ref[0:1, :] = d_bias
    sums_ref[1:2, :] = jnp.sum(d_q * gated, axis=0, keepdims=True)
    sums_ref[2:3, :] = jnp.sum(d_y * act, axis=0, keepdims=True)

    @pl.when(pair == pl.num_programs(0) - 1)
    def _():
        at_row = lax.broadcasted_iota(jnp.int32, d_scores.shape, 0)
        at_col = lax.broadcasted_iota(jnp.int32, d_scores.shape, 1)
        linked = (at_row <= at_col) & (seg_ref[...] == segt_ref[...])
        held = jnp.where(linked, d_scores[...], 0.0).astype(BF16)
        width = b_ref.shape[1]
        dbc_ref[:, :width] = plain_product(held, c_ref[...]).astype(BF16)
        dbc_ref[:, width:] = rows_product(held, b_ref[...]).astype(BF16)


def meet(barrier):
    count = lax.axis_size("tensor")
    for away in range(1, count):
        to = lax.rem(lax.axis_index("tensor") + away, count)
        pl.semaphore_signal(barrier, inc=1, device_id={"tensor": to}, device_id_type=MESH)
    pl.semaphore_wait(barrier, count - 1)


def tensor_sum_kernel(in_ref, out_ref, slots, sems):
    meet(pltpu.get_barrier_semaphore())
    copies = all_to(in_ref, slots, "tensor", sems, 0)
    for copy in copies:
        copy.start()
    total = in_ref[...]
    for away, copy in enumerate(copies):
        copy.wait()
        total = total + slots[away]
    out_ref[...] = total


def bc_conv_kernel(pre_ref, taps_ref, bias_ref, mask_ref, act_ref):
    value = conv_raw(pre_ref[...].astype(F32), taps_ref[...], bias_ref[...], mask_ref[...])
    act_ref[...] = (value * jax.nn.sigmoid(value)).astype(BF16)


def bc_back_kernel(
    d_ref, pre_ref, taps_ref, bias_ref, mask_ref, dpre_ref, dtaps_ref, dbias_ref, slots, sems
):
    count = lax.axis_size("tensor")
    me = lax.axis_index("tensor")
    cols = pre_ref.shape[1]
    slab = slots.shape[2]
    fold = slab // cols

    def place(index):
        return pl.ds(pl.multiple_of(index // fold * slab, slab), slab)

    def part(away):
        to = lax.rem(me + away, count)
        return remote(
            d_ref.at[:, place(to)], slots.at[away - 1], sems.at[0, away], sems.at[1, away],
            "tensor", to,
        )

    meet(pltpu.get_barrier_semaphore())
    for away in range(1, count):
        part(away).start()
    wide = d_ref[:, place(me)].astype(F32)
    for away in range(1, count):
        part(away).wait()
        wide = wide + slots[away - 1].astype(F32)
    d_own = wide[:, :cols]
    for piece in range(1, fold):
        d_own = jnp.where(
            me % fold == piece, wide[:, piece * cols : (piece + 1) * cols], d_own
        )
    source = pre_ref[...].astype(F32)
    value = conv_raw(source, taps_ref[...], bias_ref[...], mask_ref[...])
    d_source, d_taps, d_bias = conv_back(d_own, source, value, taps_ref[...], mask_ref[...])
    dpre_ref[...] = d_source.astype(BF16)
    dtaps_ref[...] = d_taps
    dbias_ref[...] = d_bias


MESH = pl.DeviceIdType.MESH


def lines(axis):
    count = lax.axis_size(axis)
    low = 2 if count % 2 == 0 else 1
    me = lax.axis_index(axis)
    return me, me // low, me % low, count // low, low


def remote(source, target, send, recv, axis, index):
    return pltpu.make_async_remote_copy(
        src_ref=source,
        dst_ref=target,
        send_sem=send,
        recv_sem=recv,
        device_id={axis: index},
        device_id_type=MESH,
    )


def greet_all(barrier):
    peers = 0
    for axis in ("dp", "tensor"):
        count = lax.axis_size(axis)
        for away in range(1, count):
            to = lax.rem(lax.axis_index(axis) + away, count)
            pl.semaphore_signal(barrier, inc=1, device_id={axis: to}, device_id_type=MESH)
        peers += count - 1
    pl.semaphore_wait(barrier, peers)


class Line:
    def __init__(self, axis, slot, sems):
        self.axis, self.slot, self.sems = axis, slot, sems
        self.me, self.high, self.low, self.highs, self.lows = lines(axis)

    def index(self, high, low):
        return high * self.lows + low

    def has(self, way, steps):
        if way == 0:
            return self.high - steps >= 0
        return self.high + steps < self.highs

    def towards(self, way, steps):
        return self.high - steps if way == 0 else self.high + steps

    def hop(self, way, step, low):
        block = self.slot(self.index(self.towards(way, step - 1), low))
        onto = self.index(self.towards(1 - way, 1), self.low)
        return remote(
            block, block, self.sems.at[0, way, step], self.sems.at[1, way, step], self.axis, onto
        )

    def across(self, way, steps):
        block = self.slot(self.index(self.towards(way, steps), self.low))
        onto = self.index(self.high, 1 - self.low)
        return remote(
            block, block, self.sems.at[2, way, steps], self.sems.at[3, way, steps], self.axis, onto
        )

    def sends(self, way, step):
        return self.has(1 - way, 1) & self.has(way, step - 1)

    def step(self, step):
        for way in range(2):
            if step == 0:
                pl.when(self.sends(way, 1))(lambda way=way: self.hop(way, 1, self.low).start())
                continue

            @pl.when(self.has(way, step))
            def _(way=way):
                self.hop(way, step, self.low).wait_recv()
                if step + 1 < self.highs:
                    pl.when(self.sends(way, step + 1))(
                        lambda: self.hop(way, step + 1, self.low).start()
                    )
                if self.lows == 2:
                    self.across(way, step).start()

        if step == 0 and self.lows == 2:
            self.across(0, 0).start()

    def finish(self):
        for step in range(1, self.highs):
            for way in range(2):
                pl.when(self.sends(way, step))(
                    lambda way=way, step=step: self.hop(way, step, self.low).wait_send()
                )
        if self.lows == 2:
            self.across(0, 0).wait()
            for step in range(1, self.highs):
                for way in range(2):
                    pl.when(self.has(way, step))(
                        lambda way=way, step=step: self.across(way, step).wait()
                    )


def gather_kernel(w_ref, xc_ref, wide_ref, rows_ref, dp_sems, tensor_sems, own_sems):
    deep = w_ref.shape[0]
    share = xc_ref.shape[1]

    def dp_slot(index):
        return wide_ref.at[index]

    def tensor_slot(index):
        return rows_ref.at[:, pl.ds(pl.multiple_of(index * share, share), share)]

    dp = Line("dp", dp_slot, dp_sems)
    tensor = Line("tensor", tensor_slot, tensor_sems)
    barrier = pltpu.get_barrier_semaphore()
    own = (
        pltpu.make_async_copy(w_ref, dp_slot(dp.me), own_sems.at[0]),
        pltpu.make_async_copy(xc_ref, tensor_slot(tensor.me), own_sems.at[1]),
    )
    for copy in own:
        copy.start()
    greet_all(barrier)
    for copy in own:
        copy.wait()
    for step in range(max(dp.highs, tensor.highs)):
        for line in (dp, tensor):
            if step < line.highs:
                line.step(step)
    tensor.finish()
    dp.finish()


def all_to(ref, slots, axis, sems, base):
    count = lax.axis_size(axis)
    me = lax.axis_index(axis)
    return [
        remote(
            ref, slots.at[away - 1], sems.at[0, base + away], sems.at[1, base + away], axis,
            lax.rem(me + away, count),
        )
        for away in range(1, count)
    ]


def sum_kernel(
    grads_ref, norm_ref, out_ref, small_ref, mean_ref,
    zx_ref, bc_ref, dt_ref, weight_ref, norm_share_ref, out_share_ref, small_sum_ref, gain_sum_ref,
    mean_sum_ref, share_ref, paired, held, landed, norm_slots, out_slots, small_slots, gain_slots, mean_slots, gain_ref,
    pair_sems, line_sems, norm_sems, small_sems, tensor_sems,
):
    me, high, low, highs, lows = lines("dp")
    count = lax.axis_size("dp")
    tensor_count = lax.axis_size("tensor")
    tensor_me = lax.axis_index("tensor")
    share = norm_share_ref.shape[1]
    barrier = pltpu.get_barrier_semaphore()
    greet_all(barrier)

    order = sorted(range(highs), key=lambda k: (k == 0, -min(k, highs - k)))
    partner = high * lows + (lows - 1 - low)

    def crossing(away):
        to = lax.rem(high + away, highs)
        return remote(
            grads_ref.at[to * lows + (lows - 1 - low)], paired.at[away],
            pair_sems.at[0, away], pair_sems.at[1, away], "dp", partner,
        )

    def going(away):
        to = lax.rem(high + away, highs)
        return remote(
            held.at[away], landed.at[away],
            line_sems.at[0, away], line_sems.at[1, away], "dp", to * lows + low,
        )

    def part(ref, slots, away, which):
        to = lax.rem(tensor_me + away, tensor_count)
        return remote(
            ref.at[:, pl.ds(pl.multiple_of(to * share, share), share)], slots.at[away - 1],
            norm_sems.at[0, which, away], norm_sems.at[1, which, away], "tensor", to,
        )

    small = all_to(small_ref, small_slots, "dp", small_sems, 0)
    mean = all_to(mean_ref, mean_slots, "tensor", tensor_sems, 0)
    for copy in small + mean:
        copy.start()
    if lows == 2:
        for away in order:
            crossing(away).start()
    turns = sorted(range(1, tensor_count), key=lambda k: k % 2)
    for away in turns:
        part(norm_ref, norm_slots, away, 0).start()
    for away in turns:
        part(out_ref, out_slots, away, 1).start()

    for copy in small:
        copy.wait()
    total = small_ref[...]
    for away in range(1, count):
        total = total + small_slots[away - 1]
    small_sum_ref[...] = total
    gain_rows = gain_ref.shape[0]
    gain_ref[...] = total[:gain_rows]
    gain = all_to(gain_ref, gain_slots, "tensor", tensor_sems, tensor_count)
    for copy in gain:
        copy.start()

    for away in order:
        to = lax.rem(high + away, highs)
        both = grads_ref[to * lows + low].astype(F32)
        if lows == 2:
            crossing(away).wait()
            both = both + paired[away].astype(F32)
        if away == 0:
            share_ref[...] = both
        else:
            held[away] = both.astype(BF16)
            going(away).start()

    for copy in mean + gain:
        copy.wait()
    total = mean_ref[...]
    gained = gain_ref[...]
    for away in range(1, tensor_count):
        total = total + mean_slots[away - 1]
        gained = gained + gain_slots[away - 1]
    mean_sum_ref[...] = total
    gain_sum_ref[...] = gained
    for which, ref, slots, result in (
        (0, norm_ref, norm_slots, norm_share_ref),
        (1, out_ref, out_slots, out_share_ref),
    ):
        total = ref[:, pl.ds(pl.multiple_of(tensor_me * share, share), share)].astype(F32)
        for away in range(1, tensor_count):
            part(ref, slots, away, which).wait()
            total = total + slots[away - 1].astype(F32)
        result[...] = total
    for away in order[:-1]:
        going(away).wait()
        share_ref[...] += landed[away].astype(F32)
    zx_cols, bc_cols, dt_cols = zx_ref.shape[1], bc_ref.shape[1], dt_ref.shape[1]
    zx_ref[...] = share_ref[:, :zx_cols]
    bc_ref[...] = share_ref[:, zx_cols : zx_cols + bc_cols]
    dt_ref[...] = share_ref[:, zx_cols + bc_cols : zx_cols + bc_cols + dt_cols]
    weight_ref[...] = share_ref[:, share_ref.shape[1] - weight_ref.shape[1] :]


def shape(dims, dtype=F32):
    return jax.ShapeDtypeStruct(dims, dtype)


def split_two(value):
    high = value.astype(BF16).astype(F32)
    return high, value - high


def split_three(value):
    high, rest = split_two(value)
    middle, low = split_two(rest)
    return high, middle, low


class Spread:
    def __init__(self, axis, own, slot, sems, own_sem):
        self.axis, self.own, self.slot, self.sems, self.own_sem = axis, own, slot, sems, own_sem
        self.me, self.high, self.low, self.highs, self.lows = lines(axis)

    def index(self, high, low):
        return high * self.lows + low

    def has(self, way, steps):
        if way == 0:
            return self.high - steps >= 0
        return self.high + steps < self.highs

    def towards(self, way, steps):
        return self.high - steps if way == 0 else self.high + steps

    def keep(self):
        return pltpu.make_async_copy(self.own, self.slot(self.me), self.own_sem)

    def hop(self, way, step):
        origin = self.index(self.towards(way, step - 1), self.low)
        block = self.slot(origin)
        onto = self.index(self.towards(1 - way, 1), self.low)
        return remote(
            self.own if step == 1 else block, block,
            self.sems.at[0, way, step], self.sems.at[1, way, step], self.axis, onto,
        )

    def across(self, way, steps):
        block = self.slot(self.index(self.towards(way, steps), self.low))
        onto = self.index(self.high, 1 - self.low)
        return remote(
            self.own if steps == 0 else block, block,
            self.sems.at[2, way, steps], self.sems.at[3, way, steps], self.axis, onto,
        )

    def sends(self, way, step):
        return self.has(1 - way, 1) & self.has(way, step - 1)

    def step(self, step):
        if step >= self.highs:
            return
        if step == 0:
            self.keep().start()
        for way in range(2):
            if step == 0:
                pl.when(self.sends(way, 1))(lambda way=way: self.hop(way, 1).start())
                continue

            @pl.when(self.has(way, step))
            def _(way=way):
                self.hop(way, step).wait_recv()
                if step + 1 < self.highs:
                    pl.when(self.sends(way, step + 1))(lambda: self.hop(way, step + 1).start())
                if self.lows == 2:
                    self.across(way, step).start()

        if step == 0 and self.lows == 2:
            self.across(0, 0).start()

    def finish(self):
        self.keep().wait()
        for step in range(1, self.highs):
            for way in range(2):
                pl.when(self.sends(way, step))(
                    lambda way=way, step=step: self.hop(way, step).wait_send()
                )
        if self.lows == 2:
            self.across(0, 0).wait()
            for step in range(1, self.highs):
                for way in range(2):
                    pl.when(self.has(way, step))(
                        lambda way=way, step=step: self.across(way, step).wait()
                    )


class Gradient:
    def __init__(self, send, paired, held, landed, sems):
        self.send, self.paired, self.held, self.landed, self.sems = send, paired, held, landed, sems
        self.me, self.high, self.low, self.highs, self.lows = lines("dp")

    def to(self, away):
        return lax.rem(self.high + away, self.highs)

    def theirs(self, away):
        return self.to(away) * self.lows + (self.lows - 1 - self.low)

    def mine(self, away):
        return self.to(away) * self.lows + self.low

    def cross(self, away):
        partner = self.high * self.lows + (self.lows - 1 - self.low)
        return remote(
            self.send.at[self.theirs(away)], self.paired.at[away],
            self.sems.at[0, away], self.sems.at[1, away], "dp", partner,
        )

    def going(self, away):
        return remote(
            self.held.at[away], self.landed.at[away],
            self.sems.at[2, away], self.sems.at[3, away], "dp", self.mine(away),
        )

    def fill(self, away, make):
        if self.lows == 2:
            theirs = self.theirs(away)
            self.send[theirs] = make(theirs)
            self.cross(away).start()
        mine = self.mine(away)
        self.send[mine] = make(mine)

    def both(self, away):
        both = self.send[self.mine(away)].astype(F32)
        if self.lows == 2:
            self.cross(away).wait()
            both = both + self.paired[away].astype(F32)
        return both

    def relay(self, away):
        self.held[away] = self.both(away).astype(BF16)
        self.going(away).start()

    def result(self, order):
        total = self.both(0)
        for away in order[:-1]:
            self.going(away).wait()
            total = total + self.landed[away].astype(F32)
        return total


def silu_parts(value):
    logistic = jax.nn.sigmoid(value)
    return logistic, value * logistic


def layer_kernel(
    zx_ref, x_ref, cot_ref, wo_ref, wbc_in, wdt_in, norm_in, seq_in,
    taps_in, bias_in, bct_in, bcb_in, dtb_in, alog_in, skip_in, gain_in,
    out_ref, grad_ref, gzx_ref, gside_ref, gwo_ref, gnorm_ref, gtaps_ref, gbias_ref, ggate_ref,
    gbct_ref, gbcb_ref, gdtb_ref, galog_ref, gskip_ref,
    scratch,
):
    s = SimpleNamespace(**scratch)
    fetched = (
        (wbc_in, s.wbc_in), (wdt_in, s.wdt_in), (norm_in, s.norm_in), (seq_in, s.seq_in),
        (taps_in, s.taps_in), (bias_in, s.bias_in), (bct_in, s.bct_in), (bcb_in, s.bcb_in),
        (dtb_in, s.dtb_in), (alog_in, s.alog_in), (skip_in, s.skip_in), (gain_in, s.gain_in),
    )
    fetches = [
        pltpu.make_async_copy(source, target, s.fetch_sems.at[k])
        for k, (source, target) in enumerate(fetched)
    ]
    for copy in fetches:
        copy.start()
    (
        wbc_ref, wdt_ref, norm_ref, seq_ref, taps_ref, bias_ref, bct_ref, bcb_ref, dtb_ref,
        alog_ref, skip_ref, gain_ref,
    ) = [target for _, target in fetched]
    rows, share = x_ref.shape
    inner = wo_ref.shape[1]
    side_rows, held = s.sideown.shape
    taps = taps_ref.shape[0]
    heads = skip_ref.shape[1]
    bc_cols = bct_ref.shape[1]
    tile = 128
    pairs = inner // tile
    chunks = rows // tile
    per_tile = tile // HEAD_DIM
    width = s.xr.shape[1]
    blocks = width // held
    state = s.bm.shape[1]
    gain_at = bc_cols + heads
    tensor_count = lax.axis_size("tensor")
    tensor_me = lax.axis_index("tensor")
    inner_all = inner * tensor_count

    def at(index, size=tile):
        return pl.ds(pl.multiple_of(index * size, size), size)

    def lanes(p):
        return slice(p * tile, (p + 1) * tile)

    def each_chunk(body):
        def step(c, carry):
            body(c, at(c))
            return carry

        lax.fori_loop(0, chunks, step, 0)

    def share_of(ref):
        return lambda index: ref.at[:, at(index, share)]

    def block_of(ref):
        return lambda index: ref.at[index]

    own_sems = s.own_sems
    xs = Spread("tensor", x_ref, share_of(s.xr), s.xs_sems, own_sems.at[0])
    cs = Spread("tensor", cot_ref, share_of(s.cr), s.cs_sems, own_sems.at[1])
    side = Spread("dp", s.sideown, block_of(s.side), s.side_sems, own_sems.at[2])
    wx = Spread("dp", zx_ref.at[:, inner:], block_of(s.wx), s.wx_sems, own_sems.at[3])
    wz = Spread("dp", zx_ref.at[:, :inner], block_of(s.wz), s.wz_sems, own_sems.at[4])
    wo = Spread("dp", wo_ref, block_of(s.wo), s.wo_sems, own_sems.at[5])
    highs = wx.highs
    order = list(range(highs - 1, -1, -1))

    def peers(ref, slots, sems, base=0):
        return [
            remote(
                ref, slots.at[away - 1], sems.at[0, base + away], sems.at[1, base + away],
                "tensor", lax.rem(tensor_me + away, tensor_count),
            )
            for away in range(1, tensor_count)
        ]

    greet_all(pltpu.get_barrier_semaphore())
    xs.step(0)
    wx.step(0)
    for copy in fetches:
        copy.wait()
    s.sideown[...] = jnp.concatenate(
        [
            wbc_ref[...].astype(F32), wdt_ref[...].astype(F32), norm_ref[...].astype(F32),
            jnp.zeros((side_rows - gain_at - 1, held), F32),
        ],
        axis=0,
    ).astype(BF16)
    side.step(0)
    cs.step(0)

    s.cols[...] = jnp.zeros_like(s.cols)
    s.cols[:taps, :bc_cols] = bct_ref[...]
    s.cols[taps : taps + 1, :bc_cols] = bcb_ref[...]
    s.cols[0:1, bc_cols:gain_at] = dtb_ref[...]
    s.cols[1:2, bc_cols:gain_at] = alog_ref[...]
    s.cols[...] = s.cols[...].T
    seq = seq_ref[...].astype(F32)
    at_lane = lax.broadcasted_iota(jnp.int32, (1, rows), 1)
    seq_wide = jnp.broadcast_to(seq, (tile, rows)).T
    s.seg[...] = seq_wide
    row_at = lax.broadcasted_iota(jnp.int32, (rows, tile), 0)
    for shift in range(1, taps):
        same = (pltpu.roll(seq_wide, shift, 0) == seq_wide) & (row_at >= shift)
        s.mask[shift - 1] = same.astype(F32)
    lane_masks = [None] + [
        ((pltpu.roll(seq, shift, 1) == seq) & (at_lane >= shift)).astype(F32)
        for shift in range(1, taps)
    ]
    live = (seq >= 0).astype(F32)

    def link_rows(c, held_rows):
        seg = s.seg[held_rows]
        for k in range(chunks):
            down = lax.broadcasted_iota(jnp.int32, (tile, tile), 0) + c * tile
            right = lax.broadcasted_iota(jnp.int32, (tile, tile), 1) + k * tile
            joined = (seg == seq[:, lanes(k)]) & (down >= right)
            s.link[held_rows, lanes(k)] = joined.astype(F32).astype(BF16)

    each_chunk(link_rows)
    side.step(1)
    wx.step(1)
    xs.step(1)
    side.step(2)
    wx.step(2)
    xs.finish()

    def norm_rows(c, held_rows):
        squares = jnp.zeros((tile, tile), F32)
        for k in range(width // tile):
            part = s.xr[held_rows, lanes(k)].astype(F32)
            squares = squares + part * part
        mean = jnp.sum(squares, axis=1, keepdims=True) / width
        s.inv[held_rows] = jnp.broadcast_to(lax.rsqrt(mean + EPSILON), (tile, tile))

    each_chunk(norm_rows)
    wz.step(0)
    side.step(3)
    wx.step(3)
    side.finish()
    cs.step(1)
    wo.step(0)
    for step in range(4, highs):
        side.step(step)
        wx.step(step)

    def gain_row(k):
        return s.side[k, gain_at : gain_at + 1, :].astype(F32)

    def normed_rows(c, held_rows):
        for k in range(blocks):
            here = slice(k * held, (k + 1) * held)
            inv = jnp.concatenate([s.inv[held_rows]] * (held // tile), axis=1)
            value = s.xr[held_rows, here].astype(F32) * inv * gain_row(k)
            s.normed[held_rows, here] = value.astype(BF16)

    each_chunk(normed_rows)
    side_all = jnp.concatenate([s.side[k] for k in range(blocks)], axis=1)
    side_pre = cols_product(side_all, s.normed[...])
    bc_pre = side_pre[:bc_cols].astype(BF16).astype(F32)
    s.bcpre[...] = bc_pre

    def bc_taps(k):
        return s.cols[:bc_cols, k : k + 1]

    def bc_value(source):
        value = bc_taps(taps) + bc_taps(taps - 1) * source
        for shift in range(1, taps):
            value = value + bc_taps(taps - 1 - shift) * (
                pltpu.roll(source, shift, 1) * lane_masks[shift]
            )
        return value

    value = bc_value(bc_pre)
    s.bcown[...] = silu_parts(value)[1].astype(BF16)
    bc_copies = [
        remote(
            s.bcown, s.bct.at[tensor_me], s.bc_sems.at[0, away], s.bc_sems.at[1, away],
            "tensor", lax.rem(tensor_me + away, tensor_count),
        )
        for away in range(1, tensor_count)
    ]
    for copy in bc_copies:
        copy.start()
    s.bct[tensor_me] = s.bcown[...]

    dt_in = side_pre[bc_cols:gain_at] + s.cols[bc_cols:gain_at, 0:1]
    rate = -jnp.exp(s.cols[bc_cols:gain_at, 1:2])
    step_size = jnp.maximum(dt_in, 0.0) + jnp.log1p(jnp.exp(-jnp.abs(dt_in)))
    log_decay = step_size * rate
    s.dtin[...] = dt_in
    s.ld[...] = log_decay
    zeros = jnp.zeros((heads, rows), F32)
    stacked = jnp.concatenate(split_three(log_decay) + (zeros,), axis=0).astype(BF16)
    summed = cols_product(stacked, s.link[...])
    cum = summed[:heads] + summed[heads : 2 * heads] + summed[2 * heads : 3 * heads]
    s.cum[...] = cum
    entry, tail = [], []
    for c in range(chunks):
        here = slice(c * tile, (c + 1) * tile)
        last = slice((c + 1) * tile - 1, (c + 1) * tile)
        if c == 0:
            entry.append(jnp.zeros((heads, tile), F32))
        else:
            before = slice(c * tile - 1, c * tile)
            joined = (seq[:, here] == seq[:, before]).astype(F32)
            entry.append(jnp.exp(jnp.minimum(cum[:, here] - cum[:, before], 0.0)) * joined)
        joined = (seq[:, here] == seq[:, last]).astype(F32)
        tail.append(jnp.exp(jnp.minimum(cum[:, last] - cum[:, here], 0.0)) * joined)
    parts = (cum,)
    for value in (step_size, jnp.concatenate(entry, axis=1), jnp.concatenate(tail, axis=1)):
        parts = parts + split_two(value)
    spare = jnp.zeros((tile - len(parts) * heads, rows), F32)
    columns = jnp.concatenate(parts + (spare,), axis=0).T
    s.cumc[...] = columns
    columns = columns.astype(BF16)
    row_id = lax.broadcasted_iota(jnp.int32, (tile, inner), 0)
    head_id = lax.broadcasted_iota(jnp.int32, (tile, inner), 1) // HEAD_DIM
    for k, spread in enumerate((s.stepw, s.entw, s.tailw)):
        first = heads * (1 + 2 * k)
        pick = (row_id == head_id + first) | (row_id == head_id + first + heads)
        spread[...] = plain_product(columns, pick.astype(F32).astype(BF16))

    wx.finish()

    def x_rows(c, held_rows):
        weight = s.wx[...].reshape(width, inner)
        value = plain_product(s.normed[held_rows], weight)
        s.xpre[held_rows] = value.astype(BF16).astype(F32)

    each_chunk(x_rows)
    wz.step(1)

    def mask(shift):
        return s.mask[shift - 1]

    for p in range(pairs):
        here = lanes(p)
        source = s.xpre[:, here]
        value = bias_ref[:, here] + taps_ref[taps - 1 : taps, here] * source
        for shift in range(1, taps):
            value = value + taps_ref[taps - 1 - shift : taps - shift, here] * (
                pltpu.roll(source, shift, 0) * mask(shift)
            )
        s.val[:, here] = value
        act = silu_parts(value)[1].astype(BF16).astype(F32)
        s.act[:, here] = act
        stepped = act * s.stepw[:, here]
        s.vb[:, here] = stepped.astype(BF16)
        s.xt[:, here] = (stepped * s.tailw[:, here]).astype(BF16)

    wz.step(2)
    cs.finish()
    for copy in bc_copies:
        copy.wait()
    halfway = tensor_count // 2
    bt = s.bct[:halfway].reshape(state, rows)
    ct = s.bct[halfway:].reshape(state, rows)
    s.bm[...] = bt.astype(F32).T.astype(BF16)
    s.cm[...] = ct.astype(F32).T.astype(BF16)
    wz.step(3)
    for step in range(4, highs):
        wz.step(step)
    wo.step(1)

    first_head = lax.broadcasted_iota(jnp.int32, (tile, tile), 1) < HEAD_DIM

    def two_parts(value):
        blank = jnp.zeros_like(value)
        return jnp.concatenate(
            [jnp.where(first_head, value, blank), jnp.where(first_head, blank, value)], axis=0
        )

    s.state[...] = jnp.zeros_like(s.state)

    def scan_rows(c, held_rows):
        here = at(c)
        c_rows, b_rows = s.cm[held_rows], s.bm[held_rows]
        scores = cols_product(c_rows, b_rows) * s.link[held_rows, here].astype(F32)
        prior = s.state[...].astype(BF16)
        s.prior[c] = prior
        carried = plain_product(c_rows, prior) * s.entw[held_rows]
        for p in range(pairs):
            wide = []
            for head in range(per_tile):
                h = p * per_tile + head
                spread = s.cumc[held_rows, h : h + 1] - s.cum[h : h + 1, here]
                decay = jnp.exp(jnp.minimum(spread, 0.0))
                s.decay[c, p, :, head * tile : (head + 1) * tile] = decay
                wide.append((scores * decay).astype(BF16))
            s.wst[c, p] = jnp.concatenate(wide, axis=0)
            both = two_parts(s.vb[held_rows, lanes(p)].astype(F32)).astype(BF16)
            inside = plain_product(jnp.concatenate(wide, axis=1), both)
            s.ynos[held_rows, lanes(p)] = inside + carried[:, lanes(p)]
        last = s.entw[pl.ds(c * tile + tile - 1, 1)]
        s.state[...] = s.state[...] * last + rows_product(b_rows, s.xt[held_rows])

    each_chunk(scan_rows)
    skip_wide = jnp.concatenate(
        [jnp.broadcast_to(skip_ref[:, h : h + 1], (1, HEAD_DIM)) for h in range(heads)], axis=1
    )
    wz.finish()
    wo.step(2)

    def gate_rows(c, held_rows):
        z = plain_product(s.normed[held_rows], s.wz[...].reshape(width, inner))
        squares = jnp.zeros((tile, tile), F32)
        for p in range(pairs):
            here = lanes(p)
            z_part = z[:, here].astype(BF16).astype(F32)
            s.z[held_rows, here] = z_part
            y = s.ynos[held_rows, here] + skip_wide[:, here] * s.act[held_rows, here]
            gated = y * silu_parts(z_part)[1]
            s.gated[held_rows, here] = gated
            s.q[held_rows, here] = (gated * gain_ref[:, here]).astype(BF16)
            squares = squares + gated * gated
        s.wide[held_rows] = squares

    each_chunk(gate_rows)

    def as_row(ref):
        return jnp.sum(ref[...].T, axis=0, keepdims=True)

    s.stat[0] = jnp.broadcast_to(as_row(s.wide), (8, rows))
    stat_copies = peers(s.stat.at[0], s.stat_slots.at[0], s.stat_sems)
    for copy in stat_copies:
        copy.start()
    wo.step(3)
    for step in range(4, highs):
        wo.step(step)

    def turn(k, carry):
        here = at(k)
        s.nt[here] = s.normed[:, here].astype(F32).T.astype(BF16)
        s.ct[here] = s.cr[:, here].astype(F32).T.astype(BF16)
        return carry

    lax.fori_loop(0, width // tile, turn, 0)

    def collect(copies, which):
        total = s.stat[which]
        for away, copy in enumerate(copies):
            copy.wait()
            total = total + s.stat_slots[which, away]
        return total[0:1]

    squares = collect(stat_copies, 0)
    inv_gate = lax.rsqrt(squares / inner_all + EPSILON)
    row_scale = inv_gate * live
    s.rs[...] = jnp.broadcast_to(row_scale, (tile, rows)).T

    go = Gradient(s.go_send, s.go_pair, s.go_held, s.go_land, s.go_sems)
    gz = Gradient(s.gz_send, s.gz_pair, s.gz_held, s.gz_land, s.gz_sems)
    gx = Gradient(s.gx_send, s.gx_pair, s.gx_held, s.gx_land, s.gx_sems)
    gs = Gradient(s.gs_send, s.gs_pair, s.gs_held, s.gs_land, s.gs_sems)

    def out_block(k):
        scaled = (s.ct[at(k, held)].astype(F32) * row_scale).astype(BF16)
        return plain_product(scaled, s.q[...]).astype(BF16)

    for away in order:
        go.fill(away, out_block)

    wo.finish()

    def dq_rows(c, held_rows):
        dq = plain_product(s.cr[held_rows], s.wo[...].reshape(width, inner))
        total = jnp.zeros((tile, tile), F32)
        for p in range(pairs):
            here = lanes(p)
            s.dq[held_rows, here] = dq[:, here]
            total = total + s.q[held_rows, here].astype(F32) * dq[:, here]
        s.wide[held_rows] = total

    each_chunk(dq_rows)
    s.stat[1] = jnp.broadcast_to(as_row(s.wide), (8, rows))
    stat_copies = peers(s.stat.at[1], s.stat_slots.at[1], s.stat_sems, tensor_count)
    for copy in stat_copies:
        copy.start()

    def out_part(index):
        weight = s.wo[...].reshape(width, inner)
        del weight
        return cols_product(s.q[...], wo_rows(index))

    def wo_rows(index):
        per = share // held
        return jnp.concatenate([s.wo[index * per + k] for k in range(per)], axis=0)

    def wx_rows(ref, index):
        per = share // held
        return jnp.concatenate([ref[index * per + k] for k in range(per)], axis=0)

    out_parts = (s.op_send, s.op_slots, s.op_sems)
    norm_parts = (s.np_send, s.np_slots, s.np_sems)

    def part_copy(parts, away):
        send, slots, sems = parts
        return remote(
            send.at[away], slots.at[away - 1], sems.at[0, away], sems.at[1, away],
            "tensor", lax.rem(tensor_me + away, tensor_count),
        )

    turns = sorted(range(1, tensor_count), key=lambda k: k % 2)
    for away in turns:
        s.op_send[away] = out_part(lax.rem(tensor_me + away, tensor_count)).astype(BF16)
        part_copy(out_parts, away).start()
    s.op_own[...] = out_part(tensor_me)

    inner_dot = collect(stat_copies, 1)
    pull = inv_gate * inv_gate * (inner_dot * row_scale) / inner_all
    s.pull[...] = jnp.broadcast_to(pull, (tile, rows)).T
    s.sums[...] = jnp.zeros_like(s.sums)

    def slope_rows(c, held_rows):
        scale, pulled = s.rs[held_rows], s.pull[held_rows]
        for p in range(pairs):
            here = lanes(p)
            z = s.z[held_rows, here]
            gated = s.gated[held_rows, here]
            act = s.act[held_rows, here]
            logistic, z_silu = silu_parts(z)
            y = s.ynos[held_rows, here] + skip_wide[:, here] * act
            dq = s.dq[held_rows, here] * scale
            d_gated = dq * gain_ref[:, here] - gated * pulled
            d_y = d_gated * z_silu
            d_z = d_gated * y * (logistic * (1.0 + z * (1.0 - logistic)))
            s.dz[held_rows, here] = d_z.astype(BF16)
            s.dy[held_rows, here] = d_y
            s.edy[held_rows, here] = (d_y * s.entw[held_rows, here]).astype(BF16)
            s.sums[5:6, here] += jnp.sum(dq * gated, axis=0, keepdims=True)
            s.sums[6:7, here] += jnp.sum(d_y * act, axis=0, keepdims=True)

    each_chunk(slope_rows)
    go.relay(order[0])

    def z_block(k):
        return plain_product(s.nt[at(k, held)], s.dz[...]).astype(BF16)

    for away in order:
        gz.fill(away, z_block)
        if away != order[0] and away != 0:
            go.relay(away)

    s.state[...] = jnp.zeros_like(s.state)

    def back_rows(turn, held_rows):
        c = chunks - 1 - turn
        held_rows = at(c)
        c_rows, b_rows = s.cm[held_rows], s.bm[held_rows]
        later = s.state[...].astype(BF16)
        edy = s.edy[held_rows]
        carried = plain_product(b_rows, later) * s.tailw[held_rows]
        s.dvc[held_rows] = carried
        d_scores = jnp.zeros((tile, tile), F32)
        for p in range(pairs):
            here = lanes(p)
            dy_rows = s.dy[held_rows, here].astype(BF16)
            v_both = two_parts(s.vb[held_rows, here].astype(F32)).astype(BF16)
            d_weights = cols_product(dy_rows, v_both) * s.decay[c, p]
            for head in range(per_tile):
                d_scores = d_scores + d_weights[:, head * tile : (head + 1) * tile]
            dy_both = two_parts(dy_rows.astype(F32)).astype(BF16)
            inside = rows_product(s.wst[c, p], dy_both)
            s.dv[held_rows, here] = inside
        d_scores = (d_scores * s.link[held_rows, held_rows].astype(F32)).astype(BF16)
        s.dbc[:state, held_rows] = rows_product(c_rows, d_scores) + cols_product(
            later, s.xt[held_rows]
        )
        s.dbc[state:, held_rows] = lax.dot_general(
            b_rows, d_scores, (((0,), (1,)), ((), ())), preferred_element_type=F32
        ) + cols_product(s.prior[c], edy)
        last = s.entw[pl.ds(c * tile + tile - 1, 1)]
        kept = s.state[...] * last
        through = jnp.sum(kept * s.prior[c].astype(F32), axis=0, keepdims=True)
        s.through[c] = jnp.broadcast_to(through, (8, inner))
        s.state[...] = kept + rows_product(c_rows, edy)

    each_chunk(back_rows)
    for index in range(tensor_count):
        s.dbc_send[index] = s.dbc[index * bc_cols : (index + 1) * bc_cols].astype(BF16)
    dbc_copies = [
        remote(
            s.dbc_send.at[lax.rem(tensor_me + away, tensor_count)],
            s.dbc_slots.at[away - 1], s.dbc_sems.at[0, away], s.dbc_sems.at[1, away],
            "tensor", lax.rem(tensor_me + away, tensor_count),
        )
        for away in range(1, tensor_count)
    ]
    for copy in dbc_copies:
        copy.start()

    head_row = lax.broadcasted_iota(jnp.int32, (8 * -(-heads // 8), tile), 0)
    head_lane = lax.broadcasted_iota(jnp.int32, (8 * -(-heads // 8), tile), 1) // HEAD_DIM
    d_step, d_cum, d_tail, passed = zeros, zeros, zeros, jnp.zeros((heads, 8 * chunks), F32)
    for p in range(pairs):
        here = lanes(p)
        act, d_inside, d_carried = s.act[:, here], s.dv[:, here], s.dvc[:, here]
        d_v = d_inside + d_carried
        v_part = s.vb[:, here].astype(F32)
        d_y = s.dy[:, here]
        step_wide = s.stepw[:, here]
        pick = (head_row == head_lane + p * per_tile).astype(F32).astype(BF16)
        direct = d_v * act
        turned = d_y.astype(BF16).astype(F32) * s.ynos[:, here] - v_part * d_inside
        through = jnp.concatenate([s.through[c, :, here] for c in range(chunks)], axis=0)
        for part in split_two(direct):
            d_step = d_step + cols_product(pick, part.astype(BF16))
        for part in split_three(turned):
            d_cum = d_cum + cols_product(pick, part.astype(BF16))
        for part in split_two(v_part * d_carried):
            d_tail = d_tail + cols_product(pick, part.astype(BF16))
        for part in split_two(through):
            passed = passed + cols_product(pick, part.astype(BF16))
        d_act = d_v * step_wide + skip_wide[:, here] * d_y
        source = s.xpre[:, here]
        value = s.val[:, here]
        logistic = jax.nn.sigmoid(value)
        d_value = d_act * (logistic * (1.0 + value * (1.0 - logistic)))
        d_source = taps_ref[taps - 1 : taps, here] * d_value
        s.sums[taps - 1 : taps, here] = jnp.sum(d_value * source, axis=0, keepdims=True)
        s.sums[taps : taps + 1, here] = jnp.sum(d_value, axis=0, keepdims=True)
        for shift in range(1, taps):
            kept = d_value * mask(shift)
            s.sums[taps - 1 - shift : taps - shift, here] = jnp.sum(
                kept * pltpu.roll(source, shift, 0), axis=0, keepdims=True
            )
            d_source = d_source + taps_ref[taps - 1 - shift : taps - shift, here] * pltpu.roll(
                kept, rows - shift, 0
            )
        s.dx[:, here] = d_source.astype(BF16)

    def x_block(k):
        return plain_product(s.nt[at(k, held)], s.dx[...]).astype(BF16)

    gz.relay(order[0])
    for away in order[:2]:
        gx.fill(away, x_block)
    gz.relay(order[1])

    wide = s.dbc_send[tensor_me].astype(F32)
    for away, copy in enumerate(dbc_copies):
        copy.wait()
        wide = wide + s.dbc_slots[away].astype(F32)
    source = s.bcpre[...]
    value = bc_value(source)
    logistic = jax.nn.sigmoid(value)
    d_value = wide * (logistic * (1.0 + value * (1.0 - logistic)))
    d_source = bc_taps(taps - 1) * d_value
    tap_cols = {taps - 1: d_value * source, taps: d_value}
    for shift in range(1, taps):
        kept = d_value * lane_masks[shift]
        tap_cols[taps - 1 - shift] = kept * pltpu.roll(source, shift, 1)
        d_source = d_source + bc_taps(taps - 1 - shift) * pltpu.roll(kept, rows - shift, 1)

    decays = []
    blank = jnp.zeros((heads, tile), F32)
    for c in range(chunks):
        linked = s.link[lanes(c), lanes(c)]
        ahead, behind = d_cum[:, lanes(c)], d_tail[:, lanes(c)]
        total = passed[:, 8 * c : 8 * c + 1] - behind
        for value, product in ((ahead, plain_product), (behind, cols_product)):
            stacked = jnp.concatenate(split_three(value) + (blank,), axis=0).astype(BF16)
            summed = product(stacked, linked)
            total = total + summed[:heads] + summed[heads : 2 * heads]
            total = total + summed[2 * heads : 3 * heads]
        decays.append(total)
    d_decay = jnp.concatenate(decays, axis=1)
    d_dt = (d_step[:heads] + d_decay * rate) * jax.nn.sigmoid(s.dtin[...])
    d_side = jnp.concatenate(
        [d_source, d_dt, jnp.zeros((side_rows - gain_at, rows), F32)], axis=0
    ).astype(BF16)
    s.dside[...] = d_side

    def side_block(k):
        return cols_product(s.dside[...], s.nt[at(k, held)]).astype(BF16)

    for away in order:
        gs.fill(away, side_block)
    for away in order[2:-1]:
        gx.fill(away, x_block)
        gz.relay(away)
    gx.fill(0, x_block)

    def placed(columns, height):
        lane = lax.broadcasted_iota(jnp.int32, (height, tile), 1)
        total = jnp.zeros((height, tile), F32)
        for k, column in columns.items():
            total = total + jnp.where(lane == k, jnp.sum(column, axis=1, keepdims=True), 0.0)
        return total

    small = jnp.concatenate(
        [
            placed(tap_cols, bc_cols),
            placed({0: d_dt, 1: d_decay * s.ld[...]}, heads),
            jnp.zeros((tile - gain_at, tile), F32),
        ],
        axis=0,
    ).T
    s.sums[8:16, :tile] = small[:8]

    s.meanw[...] = jnp.zeros_like(s.meanw)
    per = share // held

    def norm_part(index):
        total = cols_product(s.dz[...], wx_rows(s.wz, index))
        total = total + cols_product(s.dx[...], wx_rows(s.wx, index))
        sides = jnp.concatenate([s.side[index * per + k] for k in range(per)], axis=1)
        total = total + rows_product(s.dside[...], sides)
        here = at(index, share)
        inv = jnp.concatenate([s.inv[...]] * (share // tile), axis=1)
        weighed = total * (s.xr[:, here].astype(F32) * inv)
        gains = [gain_row(index * per + k) for k in range(per)]
        for k in range(per):
            s.gpart[index * per + k] = jnp.broadcast_to(
                jnp.sum(weighed[:, k * held : (k + 1) * held], axis=0, keepdims=True), (8, held)
            )
        rated = weighed * jnp.concatenate(gains, axis=1)
        for k in range(share // tile):
            s.meanw[...] += rated[:, lanes(k)]
        return total

    for away in turns:
        s.np_send[away] = norm_part(lax.rem(tensor_me + away, tensor_count)).astype(BF16)
        part_copy(norm_parts, away).start()
    s.np_own[...] = norm_part(tensor_me)
    s.stat[2] = jnp.broadcast_to(as_row(s.meanw), (8, rows))
    stat_copies = peers(s.stat.at[2], s.stat_slots.at[2], s.stat_sems, 2 * tensor_count)
    for copy in stat_copies:
        copy.start()
    s.sums[8:16, tile : tile + held] = jnp.concatenate(
        [s.gpart[k, 0:1] for k in range(blocks)], axis=0
    )
    pair_copy = remote(
        s.sums, s.sum_pair, s.sum_sems.at[0, 0], s.sum_sems.at[1, 0], "dp",
        gx.high * gx.lows + (gx.lows - 1 - gx.low),
    )
    if gx.lows == 2:
        pair_copy.start()
    for away in order[:2]:
        gx.relay(away)
    if gx.lows == 2:
        pair_copy.wait()
        s.sums_two[...] = s.sums[...] + s.sum_pair[...]
    else:
        s.sums_two[...] = s.sums[...]
    small_copies = [
        remote(
            s.sums_two, s.sum_slots.at[away - 1], s.sum_sems.at[0, away],
            s.sum_sems.at[1, away], "dp", gx.mine(away),
        )
        for away in range(1, highs)
    ]
    for copy in small_copies:
        copy.start()
    for away in order[:-1]:
        gs.relay(away)
    for away in order[2:-1]:
        gx.relay(away)

    gwo_ref[...] = go.result(order)
    total = s.op_own[...]
    for away in range(1, tensor_count):
        part_copy(out_parts, away).wait()
        total = total + s.op_slots[away - 1].astype(F32)
    scale = jnp.concatenate([s.rs[...]] * (share // tile), axis=1)
    here = at(tensor_me, share)
    x_own = s.xr[:, here].astype(F32)
    out_ref[...] = (x_own + total * scale).astype(BF16)
    gzx_ref[:, :inner] = gz.result(order)

    for copy in small_copies:
        copy.wait()
    total = s.sums_two[...]
    for away in range(1, highs):
        total = total + s.sum_slots[away - 1]
    gtaps_ref[...] = total[:taps]
    gbias_ref[...] = total[taps : taps + 1]
    ggate_ref[...] = total[5:6]
    gbct_ref[...] = total[8 : 8 + taps, :bc_cols]
    gbcb_ref[...] = total[8 + taps : 9 + taps, :bc_cols]
    gdtb_ref[...] = total[8:9, bc_cols:gain_at]
    galog_ref[...] = total[9:10, bc_cols:gain_at]
    lane = lax.broadcasted_iota(jnp.int32, (1, heads), 1)
    skips = jnp.zeros((1, heads), F32)
    for h in range(heads):
        part = jnp.sum(total[6:7, h * HEAD_DIM : (h + 1) * HEAD_DIM], axis=1, keepdims=True)
        skips = skips + jnp.where(lane == h, part, 0.0)
    gskip_ref[...] = skips
    s.gsum[...] = total[8:16, tile : tile + held]
    gain_copies = peers(s.gsum, s.gain_slots, s.gain_sems)
    for copy in gain_copies:
        copy.start()

    mean = collect(stat_copies, 2) / width
    mean_wide = jnp.broadcast_to(mean, (tile, rows)).T
    total = s.np_own[...]
    for away in range(1, tensor_count):
        part_copy(norm_parts, away).wait()
        total = total + s.np_slots[away - 1].astype(F32)
    own_gain = jnp.concatenate([gain_row(tensor_me * per + k) for k in range(per)], axis=1)
    inv = s.inv[...]
    pulled = jnp.concatenate([inv * mean_wide] * (share // tile), axis=1)
    inv = jnp.concatenate([inv] * (share // tile), axis=1)
    grad_ref[...] = inv * (total * own_gain - x_own * pulled) + s.cr[:, here].astype(F32)
    gains = s.gsum[...]
    for away, copy in enumerate(gain_copies):
        copy.wait()
        gains = gains + s.gain_slots[away]
    row = lax.broadcasted_iota(jnp.int32, gains.shape, 0)
    gnorm_ref[...] = jnp.sum(
        jnp.where(row == lax.axis_index("dp"), gains, 0.0), axis=0, keepdims=True
    )
    gside_ref[...] = gs.result(order)
    gzx_ref[:, inner:] = gx.result(order)


def finish_kernel(
    out_in, grad_in, gzx_in, gside_in, gwo_in, gnorm_in, gtaps_in, gbias_in, ggate_in,
    gbct_in, gbcb_in, gdtb_in, galog_in, gskip_in,
    out_ref, grad_ref, gzx_ref, gbc_ref, gdt_ref, gwo_ref, gnorm_ref, gtaps_ref, gbias_ref,
    ggate_ref, gbct_ref, gbcb_ref, gdtb_ref, galog_ref, gskip_ref,
    zx, sems,
):
    bc_cols, heads, inner = gbc_ref.shape[0], gdt_ref.shape[0], zx.shape[2]
    moves = (
        (out_in, out_ref), (grad_in, grad_ref), (gwo_in, gwo_ref),
        (gside_in.at[:bc_cols], gbc_ref), (gside_in.at[bc_cols : bc_cols + heads], gdt_ref),
        (gnorm_in, gnorm_ref), (gtaps_in, gtaps_ref), (gbias_in, gbias_ref),
        (ggate_in, ggate_ref), (gbct_in, gbct_ref), (gbcb_in, gbcb_ref), (gdtb_in, gdtb_ref),
        (galog_in, galog_ref), (gskip_in, gskip_ref), (zx, gzx_ref),
    )
    copies = [
        pltpu.make_async_copy(source, target, sems.at[k])
        for k, (source, target) in enumerate(moves)
    ]
    for copy in copies[:-1]:
        copy.start()
    for part in range(2):
        zx[:, part, :] = gzx_in[:, part * inner : (part + 1) * inner]
    copies[-1].start()
    for copy in copies:
        copy.wait()


def fused(
    x_in, cotangent, seq_ids, norm_gain, w_zx, w_bc, w_dt, w_out_t, conv_x_weight, conv_x_bias,
    conv_bc_weight, conv_bc_bias, dt_bias, a_log, d_skip, gate_gain,
):
    rows, share = x_in.shape
    held, _, inner = w_zx.shape
    bc_cols, heads, taps = w_bc.shape[1], w_dt.shape[1], conv_x_weight.shape[0]
    dp, tensor = lax.axis_size("dp"), lax.axis_size("tensor")
    highs = {name: lines(name)[3] for name in ("dp", "tensor")}
    width = share * tensor
    state = bc_cols * tensor // 2
    tile, chunks, pairs = 128, rows // 128, inner // 128
    side_rows = 16 * -(-(bc_cols + heads + 1) // 16)
    hbm = pl.BlockSpec(memory_space=pltpu.HBM)
    vmem = pl.BlockSpec(memory_space=pltpu.VMEM)

    def v(*dims, dtype=F32):
        return pltpu.VMEM(dims, dtype)

    def h(*dims):
        return pltpu.VMEM(dims, BF16)

    def sem(*dims):
        return pltpu.SemaphoreType.DMA(dims)

    high = highs["dp"]
    scratch = dict(
        xr=h(rows, width), cr=h(rows, width),
        side=h(dp, side_rows, held), wx=h(dp, held, inner), wz=h(dp, held, inner),
        wo=h(dp, held, inner),
        xs_sems=sem(4, 2, highs["tensor"]), cs_sems=sem(4, 2, highs["tensor"]),
        side_sems=sem(4, 2, high), wx_sems=sem(4, 2, high), wz_sems=sem(4, 2, high),
        wo_sems=sem(4, 2, high), own_sems=sem(6),
        seg=v(rows, tile), mask=v(taps - 1, rows, tile), link=h(rows, rows),
        inv=v(rows, tile), normed=h(rows, width), nt=h(width, rows), ct=h(width, rows),
        bcpre=v(bc_cols, rows), bcown=h(bc_cols, rows), bct=h(tensor, bc_cols, rows),
        bc_sems=sem(2, tensor), dtin=v(heads, rows), ld=v(heads, rows),
        cum=v(heads, rows), cumc=v(rows, tile),
        stepw=v(rows, inner), entw=v(rows, inner), tailw=v(rows, inner),
        xpre=v(rows, inner), val=v(rows, inner), act=v(rows, inner),
        vb=h(rows, inner), xt=h(rows, inner), bm=h(rows, state), cm=h(rows, state),
        state=v(state, inner), prior=h(chunks, state, inner),
        decay=v(chunks, pairs, tile, 2 * tile), wst=h(chunks, pairs, 2 * tile, tile),
        ynos=v(rows, inner), z=v(rows, inner), gated=v(rows, inner), q=h(rows, inner),
        wide=v(rows, tile), stat=v(3, 8, rows), stat_slots=v(3, tensor - 1, 8, rows),
        stat_sems=sem(2, 3 * tensor), rs=v(rows, tile), pull=v(rows, tile),
        dq=v(rows, inner), dz=h(rows, inner), dy=v(rows, inner), edy=h(rows, inner),
        dv=v(rows, inner), dvc=v(rows, inner), through=v(chunks, 8, inner),
        dx=h(rows, inner), dbc=v(2 * state, rows),
        dbc_send=h(tensor, bc_cols, rows), dbc_slots=h(tensor - 1, bc_cols, rows),
        dbc_sems=sem(2, tensor), dside=h(side_rows, rows), meanw=v(rows, tile),
        gpart=v(dp, 8, held), sums=v(16, inner), sums_two=v(16, inner), sum_pair=v(16, inner),
        sum_slots=v(high - 1, 16, inner),
        sum_sems=sem(2, dp), gsum=v(dp, held), gain_slots=v(tensor - 1, dp, held),
        gain_sems=sem(2, tensor),
        op_send=h(tensor, rows, share), op_slots=h(tensor - 1, rows, share),
        op_own=v(rows, share), op_sems=sem(2, tensor),
        np_send=h(tensor, rows, share), np_slots=h(tensor - 1, rows, share),
        np_own=v(rows, share), np_sems=sem(2, tensor),
        go_send=h(dp, held, inner), go_pair=h(high, held, inner), go_held=h(high, held, inner),
        go_land=h(high, held, inner), go_sems=sem(4, high),
        gz_send=h(dp, held, inner), gz_pair=h(high, held, inner), gz_held=h(high, held, inner),
        gz_land=h(high, held, inner), gz_sems=sem(4, high),
        gx_send=h(dp, held, inner), gx_pair=h(high, held, inner), gx_held=h(high, held, inner),
        gx_land=h(high, held, inner), gx_sems=sem(4, high),
        gs_send=h(dp, side_rows, held), gs_pair=h(high, side_rows, held), gs_held=h(high, side_rows, held),
        gs_land=h(high, side_rows, held), gs_sems=sem(4, high),
        sideown=h(side_rows, held), cols=v(tile, tile),
        wbc_in=h(bc_cols, held), wdt_in=h(heads, held), norm_in=h(1, held),
        seq_in=v(1, rows, dtype=jnp.int32), taps_in=v(taps, inner), bias_in=v(1, inner),
        bct_in=v(taps, bc_cols), bcb_in=v(1, bc_cols), dtb_in=v(1, heads), alog_in=v(1, heads),
        skip_in=v(1, heads), gain_in=v(1, inner), fetch_sems=sem(12),
    )
    results = pl.pallas_call(
        layer_kernel,
        in_specs=[vmem] + [hbm] * 15,
        out_specs=[vmem] * 14,
        out_shape=[
            shape((rows, share), BF16), shape((rows, share)), shape((held, 2 * inner)),
            shape((side_rows, held)), shape((held, inner)), shape((1, held)),
            shape((taps, inner)), shape((1, inner)), shape((1, inner)), shape((taps, bc_cols)),
            shape((1, bc_cols)), shape((1, heads)), shape((1, heads)), shape((1, heads)),
        ],
        scratch_shapes=[scratch],
        compiler_params=pltpu.CompilerParams(
            collective_id=0, has_side_effects=True, vmem_limit_bytes=50 * 1024 * 1024
        ),
        name="whole_layer",
    )(
        w_zx.reshape(held, 2 * inner),
        *(
            pltpu.with_memory_space_constraint(array, pltpu.HBM)
            for array in (
                x_in, cotangent, w_out_t, w_bc.T, w_dt.T, norm_gain[None, :], seq_ids[None, :],
                conv_x_weight, conv_x_bias[None, :], conv_bc_weight, conv_bc_bias[None, :],
                dt_bias[None, :], a_log[None, :], d_skip[None, :], gate_gain[None, :],
            )
        ),
    )
    finished = [
        shape((rows, share), BF16), shape((rows, share)), shape((held, 2, inner)),
        shape((bc_cols, held)), shape((heads, held)), shape((held, inner)), shape((1, held)),
        shape((taps, inner)), shape((1, inner)), shape((1, inner)), shape((taps, bc_cols)),
        shape((1, bc_cols)), shape((1, heads)), shape((1, heads)), shape((1, heads)),
    ]
    results = pl.pallas_call(
        finish_kernel,
        in_specs=[vmem] * 14,
        out_specs=[hbm] * len(finished),
        out_shape=finished,
        scratch_shapes=[v(held, 2, inner), sem(len(finished))],
        compiler_params=pltpu.CompilerParams(vmem_limit_bytes=12 * 1024 * 1024),
        name="layer_finish",
    )(*results)
    out, grad, gzx, gbc, gdt, gwo, gnorm, gtaps, gbias, ggate, gbct, gbcb, gdtb, galog, gskip = (
        results
    )
    return (
        out, grad, gnorm[0], gzx, gbc.T, gdt.T, gwo, gtaps, gbias[0], gbct, gbcb[0], gdtb[0],
        galog[0], gskip[0], ggate[0],
    )


def fits(x_in, w_zx, w_bc, w_dt, w_out_t, taps, tensor_count):
    rows, share = x_in.shape
    held, inner = w_out_t.shape
    bc_cols, heads = w_bc.shape[1], w_dt.shape[1]
    dp_count = lax.axis_size("dp")
    return (
        held == 128 and share % held == 0 and rows % 128 == 0 and inner % 128 == 0
        and dp_count == 8 and heads == 8 and bc_cols % 16 == 0 and taps == 4
        and tensor_count % 2 == 0 and bc_cols * tensor_count == 256
        and inner == heads * HEAD_DIM
    )


def local(
    x_in,
    cotangent,
    seq_ids,
    norm_gain,
    w_zx,
    w_bc,
    w_dt,
    w_out_t,
    conv_x_weight,
    conv_x_bias,
    conv_bc_weight,
    conv_bc_bias,
    dt_bias,
    a_log,
    d_skip,
    gate_gain,
    *,
    tensor_count,
):
    if fits(x_in, w_zx, w_bc, w_dt, w_out_t, conv_x_weight.shape[0], tensor_count):
        return fused(
            x_in, cotangent, seq_ids, norm_gain, w_zx, w_bc, w_dt, w_out_t, conv_x_weight, conv_x_bias,
            conv_bc_weight, conv_bc_bias, dt_bias, a_log, d_skip, gate_gain,
        )
    rows, share = x_in.shape
    width = share * tensor_count
    inner = w_out_t.shape[1]
    pairs = inner // PAIR
    heads = w_dt.shape[1]
    bc_cols = w_bc.shape[1]
    taps = conv_x_weight.shape[0]
    held_rows = w_zx.shape[0]
    spare = -(bc_cols + heads + 1) % 128
    side = bc_cols + heads + 1 + spare

    counts = {name: lax.axis_size(name) for name in ("dp", "tensor")}
    highs = {name: -(-counts[name] // 2) if counts[name] % 2 == 0 else counts[name] for name in counts}
    vmem = pl.BlockSpec(memory_space=pltpu.VMEM)
    local_weights = jnp.concatenate(
        [
            w_zx.reshape(held_rows, -1),
            w_bc,
            w_dt,
            norm_gain[:, None],
            jnp.zeros((held_rows, spare), BF16),
            w_out_t,
        ],
        axis=1,
    )
    packs = local_weights.shape[1]
    gathered, both = pl.pallas_call(
        gather_kernel,
        in_specs=[vmem, vmem],
        out_specs=[vmem, vmem],
        out_shape=[
            shape((counts["dp"], held_rows, packs), BF16),
            shape((2 * rows, width), BF16),
        ],
        scratch_shapes=[
            pltpu.SemaphoreType.DMA((4, 2, highs["dp"])),
            pltpu.SemaphoreType.DMA((4, 2, highs["tensor"])),
            pltpu.SemaphoreType.DMA((2,)),
        ],
        compiler_params=pltpu.CompilerParams(collective_id=0, has_side_effects=True),
        name="opening_gather",
    )(local_weights, jnp.concatenate([x_in, cotangent], axis=0))
    gathered = gathered.reshape(counts["dp"] * held_rows, packs)
    packed = gathered[:, : 2 * inner + side]
    out_weight = gathered[:, 2 * inner + side :]

    x_rows, cot_rows = both[:rows], both[rows:]
    col_start = lax.axis_index("tensor") * share
    live = (seq_ids >= 0).astype(F32)
    masks = [live[:, None]]
    for shift in range(1, taps):
        same = (seq_ids[shift:] == seq_ids[:-shift]).astype(F32)
        masks.append(jnp.concatenate([jnp.zeros((shift,), F32), same])[:, None])
    masks = jnp.concatenate(masks, axis=1)
    seg, segt = seq_ids[:, None], seq_ids[None, :]

    gain = packed[:, 2 * inner + bc_cols + heads].astype(F32)
    x_float = x_rows.astype(F32)
    inv_rms = lax.rsqrt(jnp.mean(x_float * x_float, axis=-1) + EPSILON)
    normed = (x_float * inv_rms[:, None] * gain[None, :]).astype(BF16)
    zx = plain_product(normed, packed[:, : 2 * inner]).astype(BF16)
    bcdt = plain_product(normed, packed[:, 2 * inner :])
    bc_pre = bcdt[:, :bc_cols].astype(BF16)
    dt_in = bcdt[:, bc_cols : bc_cols + heads] + dt_bias[None, :]

    bc_local = pl.pallas_call(
        bc_conv_kernel, out_shape=shape((rows, bc_cols), BF16), name="bc_conv"
    )(bc_pre, conv_bc_weight, conv_bc_bias[None, :], masks)
    bc_act = lax.all_gather(bc_local, "tensor", axis=1, tiled=True)
    state = bc_act.shape[1] // 2
    b_matrix, c_matrix = bc_act[:, :state], bc_act[:, state:]

    step = jax.nn.softplus(dt_in)
    rate = -jnp.exp(a_log)
    log_decay = step * rate[None, :]
    at = jnp.arange(rows)
    lower = (at[:, None] >= at[None, :]).astype(F32)
    cumulative = jnp.dot(lower, log_decay, precision=PRECISE)
    step_pairs = step.reshape(rows, pairs, 2).transpose(1, 0, 2)
    cum_pairs = cumulative.reshape(rows, pairs, 2).transpose(1, 0, 2)
    cumt_pairs = cumulative.T.reshape(pairs, 2, rows)
    skip_wide = jnp.repeat(d_skip, HEAD_DIM)[None, :]
    gate_wide = gate_gain[None, :]
    d_q_raw = plain_product(cot_rows, out_weight)

    def whole(dims):
        return pl.BlockSpec(dims, lambda p: (0,) * len(dims))

    columns = pl.BlockSpec((rows, PAIR), lambda p: (0, p))
    row_wide = pl.BlockSpec((1, PAIR), lambda p: (0, p))
    per_pair = pl.BlockSpec((1, rows, 2), lambda p: (p, 0, 0))
    per_pair_t = pl.BlockSpec((1, 2, rows), lambda p: (p, 0, 0))
    common_specs = [
        columns,
        pl.BlockSpec((rows, PAIR), lambda p: (0, p + pairs)),
        whole((rows, state)),
        whole((rows, state)),
        pl.BlockSpec((taps, PAIR), lambda p: (0, p)),
        row_wide,
        whole((rows, taps)),
        whole((rows, 1)),
        whole((1, rows)),
        per_pair,
        per_pair,
        per_pair_t,
        row_wide,
        row_wide,
        columns,
    ]
    common = (
        zx, zx, b_matrix, c_matrix, conv_x_weight, conv_x_bias[None, :], masks, seg, segt,
        step_pairs, cum_pairs, cumt_pairs, skip_wide, gate_wide, d_q_raw,
    )
    x_act, y_flat, q_rows, stats = pl.pallas_call(
        forward_kernel,
        grid=(pairs,),
        in_specs=common_specs,
        out_specs=[columns, columns, columns, whole((rows, 2))],
        out_shape=[
            shape((rows, inner), BF16),
            shape((rows, inner)),
            shape((rows, inner), BF16),
            shape((rows, 2)),
        ],
        scratch_shapes=[pltpu.VMEM((rows, rows), F32)],
        name="mixer_forward",
    )(*common)

    stat_dims = (2 * rows // 128, 128)
    totals = pl.pallas_call(
        tensor_sum_kernel,
        out_shape=shape(stat_dims),
        in_specs=[vmem],
        out_specs=vmem,
        scratch_shapes=[
            pltpu.VMEM((counts["tensor"] - 1,) + stat_dims, F32),
            pltpu.SemaphoreType.DMA((2, counts["tensor"])),
        ],
        compiler_params=pltpu.CompilerParams(collective_id=2, has_side_effects=True),
        name="stat_sum",
    )(stats.T.reshape(stat_dims)).reshape(2, rows)
    partial_out = cols_product(q_rows, out_weight).astype(BF16)
    inner_all = inner * tensor_count
    inv_gate = lax.rsqrt(totals[0] / inner_all + EPSILON)
    row_scale = inv_gate * live
    pull = inv_gate * inv_gate * (totals[1] * row_scale) / inner_all
    scales = jnp.stack([row_scale, pull], axis=1)
    d_scaled = (cot_rows.astype(F32) * row_scale[:, None]).astype(BF16)
    out_grad = rows_product(d_scaled, q_rows).astype(BF16)

    d_z, d_x, d_bc, d_taps, sums, d_step, rowsum, colsum = pl.pallas_call(
        backward_kernel,
        grid=(pairs,),
        in_specs=common_specs + [columns, columns, whole((rows, 2))],
        out_specs=[
            columns,
            columns,
            whole((rows, 2 * state)),
            pl.BlockSpec((taps, PAIR), lambda p: (0, p)),
            pl.BlockSpec((3, PAIR), lambda p: (0, p)),
            per_pair,
            per_pair_t,
            per_pair,
        ],
        out_shape=[
            shape((rows, inner), BF16),
            shape((rows, inner), BF16),
            shape((rows, 2 * state), BF16),
            shape((taps, inner)),
            shape((3, inner)),
            shape((pairs, rows, 2)),
            shape((pairs, 2, rows)),
            shape((pairs, rows, 2)),
        ],
        scratch_shapes=[pltpu.VMEM((rows, rows), F32), pltpu.VMEM((rows, rows), F32)],
        name="mixer_backward",
    )(*common, x_act, y_flat, scales)

    slab = max(bc_cols, 128)
    d_cum = rowsum.reshape(heads, rows).T - colsum.transpose(1, 0, 2).reshape(rows, heads)
    d_decay = lax.dot_general(lower, d_cum, (((0,), (0,)), ((), ())), precision=PRECISE)
    d_step_all = d_step.transpose(1, 0, 2).reshape(rows, heads) + d_decay * rate[None, :]
    d_dt = d_step_all * jax.nn.sigmoid(dt_in)
    d_bcpre, bc_taps_grad, bc_bias_grad = pl.pallas_call(
        bc_back_kernel,
        out_shape=[
            shape((rows, bc_cols), BF16),
            shape((taps, bc_cols)),
            shape((1, bc_cols)),
        ],
        in_specs=[vmem] * 5,
        out_specs=[vmem] * 3,
        scratch_shapes=[
            pltpu.VMEM((counts["tensor"] - 1, rows, slab), BF16),
            pltpu.SemaphoreType.DMA((2, counts["tensor"])),
        ],
        compiler_params=pltpu.CompilerParams(collective_id=3, has_side_effects=True),
        name="bc_conv_back",
    )(d_bc, bc_pre, conv_bc_weight, conv_bc_bias[None, :], masks)

    d_side = jnp.concatenate(
        [d_z, d_x, d_bcpre, d_dt.astype(BF16), jnp.zeros((rows, side - bc_cols - heads), BF16)],
        axis=1,
    )
    pack_grad = rows_product(normed, d_side).astype(BF16)
    d_norm_part = cols_product(d_side, packed)
    x_hat = x_float * inv_rms[:, None]
    weighed = d_norm_part * x_hat
    gain_part = jnp.sum(weighed, axis=0)
    mean_part = jnp.sum(weighed * gain[None, :], axis=1)
    pieces = (
        gain_part,
        d_taps.reshape(-1),
        sums[0],
        bc_taps_grad.reshape(-1),
        bc_bias_grad[0],
        jnp.sum(d_dt, axis=0),
        jnp.sum(d_decay * log_decay, axis=0),
        jnp.sum(sums[2].reshape(heads, HEAD_DIM), axis=1),
        sums[1],
    )
    length = sum(piece.shape[0] for piece in pieces)
    lane = 128
    depth = 8 * -(-length // (8 * lane))
    flat = jnp.concatenate(pieces + (jnp.zeros((depth * lane - length,), F32),))
    gain_rows = width // lane
    mean_rows = -(-rows // lane)
    grads = jnp.concatenate([pack_grad, out_grad], axis=1).reshape(counts["dp"], held_rows, packs)
    dp_high, dp_others, tensor_others = highs["dp"], counts["dp"] - 1, counts["tensor"] - 1
    zx_share, bc_share, dt_share, out_grad_share, d_norm_own, out_share, flat, gain_sum, mean_sum = pl.pallas_call(
        sum_kernel,
        in_specs=[vmem] * 5,
        out_specs=[vmem] * 9,
        out_shape=[
            shape((held_rows, 2 * inner)),
            shape((held_rows, bc_cols)),
            shape((held_rows, heads)),
            shape((held_rows, inner)),
            shape((rows, share)),
            shape((rows, share)),
            shape((depth, lane)),
            shape((gain_rows, lane)),
            shape((mean_rows, lane)),
        ],
        scratch_shapes=[
            pltpu.VMEM((held_rows, packs), F32),
            pltpu.VMEM((dp_high, held_rows, packs), BF16),
            pltpu.VMEM((dp_high, held_rows, packs), BF16),
            pltpu.VMEM((dp_high, held_rows, packs), BF16),
            pltpu.VMEM((tensor_others, rows, share), BF16),
            pltpu.VMEM((tensor_others, rows, share), BF16),
            pltpu.VMEM((dp_others, depth, lane), F32),
            pltpu.VMEM((tensor_others, gain_rows, lane), F32),
            pltpu.VMEM((tensor_others, mean_rows, lane), F32),
            pltpu.VMEM((gain_rows, lane), F32),
            pltpu.SemaphoreType.DMA((2, dp_high)),
            pltpu.SemaphoreType.DMA((2, dp_high)),
            pltpu.SemaphoreType.DMA((2, 2, tensor_others + 1)),
            pltpu.SemaphoreType.DMA((2, dp_others + 1)),
            pltpu.SemaphoreType.DMA((2, 2 * tensor_others + 2)),
        ],
        compiler_params=pltpu.CompilerParams(collective_id=1, has_side_effects=True),
        name="closing_sums",
    )(
        grads,
        d_norm_part.astype(BF16),
        partial_out,
        flat.reshape(depth, lane),
        mean_part.reshape(mean_rows, lane),
    )
    output = (x_in.astype(F32) + out_share * row_scale[:, None]).astype(BF16)
    row_mean = mean_sum.reshape(-1) / width
    gain_own = lax.dynamic_slice_in_dim(gain, col_start, share, 0)
    input_grad = inv_rms[:, None] * (
        d_norm_own * gain_own[None, :]
        - x_in.astype(F32) * (inv_rms * row_mean)[:, None]
    ) + cotangent.astype(F32)
    flat = flat.reshape(-1)
    parts, at_piece = [], 0
    for piece in pieces:
        parts.append(flat[at_piece : at_piece + piece.shape[0]])
        at_piece += piece.shape[0]
    parts = parts[1:]
    gain_share = lax.dynamic_slice_in_dim(
        gain_sum.reshape(-1), lax.axis_index("dp") * held_rows, held_rows, 0
    )
    return (
        output,
        input_grad,
        gain_share,
        zx_share.reshape(held_rows, 2, inner),
        bc_share,
        dt_share,
        out_grad_share,
        parts[0].reshape(taps, inner),
        parts[1],
        parts[2].reshape(taps, bc_cols),
        parts[3],
        parts[4],
        parts[5],
        parts[6],
        parts[7],
    )


def solution(mesh):
    return jax.shard_map(
        partial(local, tensor_count=mesh.shape["tensor"]),
        mesh=mesh,
        in_specs=(
            P("dp", "tensor"),
            P("dp", "tensor"),
            P("dp"),
            P("dp"),
            P("dp", None, "tensor"),
            P("dp", "tensor"),
            P("dp", "tensor"),
            P("dp", "tensor"),
            P(None, "tensor"),
            P("tensor"),
            P(None, "tensor"),
            P("tensor"),
            P("tensor"),
            P("tensor"),
            P("tensor"),
            P("tensor"),
        ),
        out_specs=(
            P("dp", "tensor"),
            P("dp", "tensor"),
            P("dp"),
            P("dp", None, "tensor"),
            P("dp", "tensor"),
            P("dp", "tensor"),
            P("dp", "tensor"),
            P(None, "tensor"),
            P("tensor"),
            P(None, "tensor"),
            P("tensor"),
            P("tensor"),
            P("tensor"),
            P("tensor"),
            P("tensor"),
        ),
        check_vma=False,
    )
```
